512 devices in a mesh: grp: 16 (over y, core), mdl: 32 (over x, z).
Axes of the slice: x: 4, y: 8, z: 8, core: 2. Of those that a mesh axis runs over, the one named last changes fastest.
Arguments:
- row_states: bfloat16 [6144, 1024], P('grp', 'mdl'), may hold values from -6 to 6
- ffn_gain: bfloat16 [1024], replicated, may hold values from 0.25 to 1.75
- ffn_in: bfloat16 [1024, 32768], P('grp', 'mdl'), may hold values from -0.1875 to 0.1875
- ffn_out: bfloat16 [32768, 1024], P('mdl', 'grp'), may hold values from -0.0625 to 0.0625
- final_gain: bfloat16 [1024], replicated, may hold values from 0.25 to 1.75
- kv_weight: bfloat16 [2, 1024, 16384], P(None, None, 'mdl'), may hold values from -0.1875 to 0.1875
- queries: bfloat16 [4096, 16384], P('grp', 'mdl'), may hold values from -36 to 36
- attn_out: bfloat16 [16384, 1024], P('mdl'), may hold values from -0.75 to 0.75
- row_question: int32 [6144], replicated, may hold values from 0 to 15, as said below
Outputs:
- cross_out: bfloat16 [4096, 1024], P(('grp', 'mdl'))
The draws below stay inside these ranges and needn't reach their ends.
Inputs may be any that keep to these rules, and one draw needn't show every extreme that they name: `row_question`: within each block of 384 rows (one row group) the rows are sorted by question; in every block each question owns a multiple of 8 rows, at least 8 and at most 72, and one question, drawn from the seed, owns exactly 72 rows of every block.
All inputs are finite; a program needn't handle non-finite values.
Results may differ from the reference program's by a relative error of at most 0.029.
Values may be sent and summed in bfloat16 or wider, within the bound.
No kernel may reach another device: no remote copies, remote signals or barrier semaphores. Data moves between devices by JAX's collectives and lax.ppermute only.
A program may use at most 64 MiB of HBM per device.

```python
import jax
import jax.numpy as jnp
from jax import lax

D = 1024
FF = 32768
HEADS = 128
HEAD_DIM = 128
R_GRP = 384
TGT = 256
ROWS = 6144
N_GRP = 16


def draw_queries(key, part):
    shape = (N_GRP * TGT, HEADS * HEAD_DIM)
    base = jnp.clip(jax.random.normal(key, shape, jnp.float32), -6.0, 6.0)
    return (base * 0.1).astype(jnp.bfloat16)


def draw_row_question(key, part):
    units = R_GRP // 8
    per_owner = units // N_GRP
    slots_each = 3 * per_owner
    slot_total = N_GRP * slots_each
    weights = jax.random.randint(jax.random.fold_in(key, 11), (N_GRP,), 1, 4)
    heavy = jax.random.randint(jax.random.fold_in(key, 12), (), 0, N_GRP)
    weights = jnp.where(jnp.arange(N_GRP) == heavy, 3, weights)
    slot_owner = jnp.arange(slot_total) // slots_each
    slot_rank = jnp.arange(slot_total) % slots_each
    usable = slot_rank < weights[slot_owner] * per_owner
    forced = (slot_owner == heavy) | (slot_rank == 0)

    def one_group(group_key):
        order = jax.random.permutation(group_key, slot_total)
        score = order + jnp.where(forced, 0, slot_total) + jnp.where(usable, 0, 2 * slot_total)
        ranking = jnp.argsort(jnp.argsort(score, stable=True), stable=True)
        taken = (ranking < units).astype(jnp.int32)
        counts = jnp.sum(taken.reshape(N_GRP, slots_each), axis=1) * 8
        bounds = jnp.cumsum(counts)
        positions = jnp.arange(R_GRP)
        return jnp.sum((positions[:, None] >= bounds[None, :]).astype(jnp.int32), axis=1)
    group_keys = jax.random.split(jax.random.fold_in(key, 13), N_GRP)
    return jax.vmap(one_group)(group_keys).reshape(N_GRP * R_GRP).astype(jnp.int32)


def spiked(array, rng, source, target, parts, factor):
    owner, partner = [(jnp.arange(array.shape[dim]) // (array.shape[dim] // parts)).reshape([-1 if axis == dim else 1 for axis in range(array.ndim)]) for dim in (source, target)]
    chosen = jax.random.permutation(rng, parts)[partner]
    strong = (owner == chosen) | (owner == (partner + parts // 2) % parts)
    return jnp.where(strong, factor * array, array)


def levels(rng, shape, cuts, smallest, top_value):
    loudness = 1.0
    for position, parts in cuts:
        draws = jax.random.uniform(jax.random.fold_in(jax.random.fold_in(rng, 6), position), (parts,), jnp.float32, smallest / len(cuts), top_value / len(cuts))
        loudness = loudness * jnp.repeat(jnp.exp(draws), shape[position] // parts).reshape((-1,) + (1,) * (len(shape) - 1 - position))
    return loudness


def gaussian(own_key, dims, deviation, reach, shards=(), held_as=jnp.bfloat16):
    drawn = deviation * jax.random.normal(own_key, dims, jnp.float32)
    if shards:
        drawn = drawn * levels(own_key, dims, shards, -0.22, 0.18)
    return jnp.clip(drawn, -reach, reach).astype(held_as)


def noise_with(key, dims, deviation, reach, pieces, heavy, kind=jnp.bfloat16):
    values = deviation * jax.random.normal(key, dims, jnp.float32)
    if pieces:
        values = values * levels(key, dims, pieces, -0.22, 0.18)
    return jnp.clip(spiked(values, jax.random.fold_in(key, 3), *heavy), -reach, reach).astype(kind)


def setup_inputs(seed: int = 0) -> dict:
    seeds = jax.random.split(jax.random.key(seed), 10)
    row_states = gaussian(seeds[0], (ROWS, D), 1.0, 6.0, ((0, 16), (1, 32)))
    ffn_gain = jnp.clip(1.0 + 0.15 * jax.random.normal(seeds[1], (D,), jnp.float32), 0.25, 1.75).astype(jnp.bfloat16)
    ffn_in = gaussian(seeds[2], (D, FF), D ** -0.5, 0.1875, ((0, 16), (1, 32)))
    ffn_out = noise_with(seeds[3], (FF, D), FF ** -0.5, 0.0625, ((0, 32), (1, 16)), (0, 1, 32, 2.75))
    final_gain = jnp.clip(1.0 + 0.15 * jax.random.normal(seeds[4], (D,), jnp.float32), 0.25, 1.75).astype(jnp.bfloat16)
    kv_weight = gaussian(seeds[5], (2, D, HEADS * HEAD_DIM), D ** -0.5, 0.1875, ((2, 32),))
    queries = draw_queries(jax.random.fold_in(seeds[9], 71), 0)
    attn_out = gaussian(seeds[7], (HEADS * HEAD_DIM, D), (HEAD_DIM // 2) ** -0.5, 0.75, ((0, 32),))
    row_question = draw_row_question(jax.random.fold_in(seeds[9], 71), 0)
    return dict(row_states=row_states, ffn_gain=ffn_gain, ffn_in=ffn_in, ffn_out=ffn_out, final_gain=final_gain, kv_weight=kv_weight, queries=queries, attn_out=attn_out, row_question=row_question)


def rms_normalize(states, gain):
    wide = states.astype(jnp.float32)
    factor = lax.rsqrt(lax.optimization_barrier(jnp.mean(wide * wide, axis=-1, keepdims=True)) + 1e-06)
    return (wide * factor * gain.astype(jnp.float32)).astype(jnp.bfloat16)

def reference(row_states, ffn_gain, ffn_in, ffn_out, final_gain, kv_weight, queries, attn_out, row_question):
    normed = rms_normalize(row_states, ffn_gain)
    hidden = jnp.maximum(jnp.dot(normed, ffn_in, preferred_element_type=jnp.float32), 0.0).astype(jnp.bfloat16)
    ffn_sum = jnp.dot(hidden, ffn_out, preferred_element_type=jnp.float32)
    enc_state = (row_states.astype(jnp.float32) + ffn_sum).astype(jnp.bfloat16)
    encoded = rms_normalize(enc_state, final_gain)
    key_rows = jnp.dot(encoded, kv_weight[0], preferred_element_type=jnp.float32).astype(jnp.bfloat16)
    value_rows = jnp.dot(encoded, kv_weight[1], preferred_element_type=jnp.float32).astype(jnp.bfloat16)
    capacity = 3 * R_GRP // N_GRP
    owners = row_question.reshape(N_GRP, R_GRP)
    owner_table = (owners[:, :, None] == jnp.arange(N_GRP, dtype=jnp.int32)[None, None, :]).astype(jnp.int32)
    counts = lax.optimization_barrier(jnp.sum(owner_table, axis=1))
    starts = jnp.cumsum(counts, axis=1) - counts
    slot_index = jnp.arange(capacity, dtype=jnp.int32)
    group_base = jnp.arange(N_GRP, dtype=jnp.int32) * R_GRP

    def one_question(question):
        owned = counts[:, question]
        begin = starts[:, question]
        is_valid = (slot_index[None, :] < owned[:, None]).reshape(-1)
        picks = jnp.minimum(group_base[:, None] + begin[:, None] + slot_index[None, :], N_GRP * R_GRP - 1).reshape(-1).astype(jnp.int32)
        keys_here = jnp.take(key_rows, picks, axis=0).astype(jnp.float32).reshape(-1, HEADS, HEAD_DIM)
        values_here = jnp.take(value_rows, picks, axis=0).astype(jnp.float32).reshape(-1, HEADS, HEAD_DIM)
        asked = lax.dynamic_slice_in_dim(queries, (question * TGT).astype(jnp.int32), TGT, 0)
        asked = asked.astype(jnp.float32).reshape(TGT, HEADS, HEAD_DIM)
        scores = jnp.einsum('thd,rhd->htr', asked, keys_here)
        scores = jnp.where(is_valid[None, None, :], scores, -1e+30)
        top_score = lax.optimization_barrier(jnp.max(scores, axis=-1, keepdims=True))
        raised = jnp.where(is_valid[None, None, :], jnp.exp(scores - top_score), 0.0)
        probabilities = (raised / lax.optimization_barrier(jnp.sum(raised, axis=-1, keepdims=True))).astype(jnp.bfloat16)
        attended = jnp.einsum('htr,rhd->thd', probabilities.astype(jnp.float32), values_here)
        attended = attended.astype(jnp.bfloat16).reshape(TGT, HEADS * HEAD_DIM)
        return jnp.dot(attended, attn_out, preferred_element_type=jnp.float32).astype(jnp.bfloat16)
    outputs = lax.map(one_question, jnp.arange(N_GRP, dtype=jnp.int32))
    return outputs.reshape(N_GRP * TGT, D)
```

```python
import jax
import jax.numpy as jnp
from jax import lax
from jax.sharding import Mesh, PartitionSpec as P

HEAD_DIM = 128
GRP = ("y", "core")
MDL = ("x", "z")


def swap_cores(value):
    return lax.ppermute(value, "core", [(0, 1), (1, 0)])


def normalize_columns(states, gain):
    wide = states.astype(jnp.float32)
    factor = lax.rsqrt(jnp.mean(wide * wide, axis=0, keepdims=True) + 1e-06)
    return (wide * factor * gain.astype(jnp.float32)[:, None]).astype(jnp.bfloat16)


def slot_plan(row_question, rows_local, groups, my_group):
    capacity = 3 * rows_local // groups
    owners = row_question.reshape(groups, rows_local)
    questions = jnp.arange(groups, dtype=jnp.int32)
    counts = jnp.sum((owners[:, :, None] == questions).astype(jnp.int32), axis=1)
    slots = jnp.arange(capacity, dtype=jnp.int32)
    mine = lax.dynamic_index_in_dim(owners, my_group, 0, keepdims=False)
    sent_counts = lax.dynamic_index_in_dim(counts, my_group, 0, keepdims=False)
    sent_starts = jnp.sum((mine[None, :] < questions[:, None]).astype(jnp.int32), axis=1)
    source = jnp.where(
        slots[None, :] < sent_counts[:, None], sent_starts[:, None] + slots[None, :], -1
    )
    got_counts = lax.dynamic_index_in_dim(counts, my_group, 1, keepdims=False)
    got_valid = (slots[None, :] < got_counts[:, None]).reshape(-1)
    rows = jnp.arange(rows_local, dtype=jnp.int32)
    pick = (rows[:, None] == source.reshape(1, -1)).astype(jnp.bfloat16)
    return capacity, pick, got_valid


def local(
    row_states, ffn_gain, ffn_in, ffn_out, final_gain, kv_weight, queries, attn_out, row_question
):
    groups = lax.axis_size(GRP)
    models = lax.axis_size(MDL)
    my_group = lax.axis_index(GRP)
    my_core = lax.axis_index("core")
    rows_local, feats_local = row_states.shape
    hid_local = ffn_in.shape[1]
    width = feats_local * models

    own_rows = row_states.T
    in_half = lax.all_gather(ffn_in, "y", axis=0, tiled=True)
    in_other = swap_cores(in_half)
    out_half = lax.all_gather(ffn_out.T, "y", axis=0, tiled=True)
    out_other = swap_cores(out_half)
    full_rows = lax.all_gather(own_rows, MDL, axis=0, tiled=True)
    normed = normalize_columns(full_rows, ffn_gain)
    halves = normed.reshape(-1, 2, ffn_in.shape[0], rows_local)
    mine = lax.dynamic_index_in_dim(halves, my_core, 1, keepdims=False).reshape(-1, rows_local)
    theirs = lax.dynamic_index_in_dim(halves, 1 - my_core, 1, keepdims=False)
    theirs = theirs.reshape(-1, rows_local)

    def contract(weight, columns):
        return lax.dot_general(
            weight, columns, (((0,), (0,)), ((), ())), preferred_element_type=jnp.float32
        )

    pre_active = contract(in_half, mine) + contract(in_other, theirs)
    hidden = jnp.maximum(pre_active, 0.0).astype(jnp.bfloat16)
    share_mine = jnp.dot(out_half, hidden, preferred_element_type=jnp.float32)
    share_other = jnp.dot(out_other, hidden, preferred_element_type=jnp.float32)
    share_mine = share_mine.astype(jnp.bfloat16).reshape(-1, 1, ffn_out.shape[1], rows_local)
    share_other = share_other.astype(jnp.bfloat16).reshape(-1, 1, ffn_out.shape[1], rows_local)
    first = my_core == 0
    shares = jnp.concatenate(
        [
            jnp.where(first, share_mine, share_other),
            jnp.where(first, share_other, share_mine),
        ],
        axis=1,
    ).reshape(models, feats_local, rows_local)
    arrived = lax.all_to_all(shares, MDL, 0, 0, tiled=True)
    ffn_sum = jnp.sum(arrived.astype(jnp.float32), axis=0)
    enc_state = (own_rows.astype(jnp.float32) + ffn_sum).astype(jnp.bfloat16)

    capacity, pick, got_valid = slot_plan(row_question, rows_local, groups, my_group)
    packed = jnp.dot(enc_state, pick, preferred_element_type=jnp.float32).astype(jnp.bfloat16)
    packed = packed.reshape(feats_local, groups, capacity).transpose(1, 0, 2)
    regrouped = lax.all_to_all(packed, GRP, 0, 0, tiled=True)
    slots = regrouped.transpose(1, 0, 2).reshape(feats_local, groups * capacity)
    slot_rows = lax.all_gather(slots, MDL, axis=0, tiled=True)
    encoded = normalize_columns(slot_rows, final_gain)

    projected = lax.dot_general(
        kv_weight, encoded, (((1,), (0,)), ((), ())), preferred_element_type=jnp.float32
    ).astype(jnp.bfloat16)
    head_cols = kv_weight.shape[2]
    heads_local = head_cols // HEAD_DIM
    targets = queries.shape[0]
    key_heads = projected[0].reshape(heads_local, HEAD_DIM, -1)
    value_heads = projected[1].reshape(heads_local, HEAD_DIM, -1)
    query_heads = queries.reshape(targets, heads_local, HEAD_DIM)
    scores = jnp.einsum("thd,hdr->htr", query_heads, key_heads, preferred_element_type=jnp.float32)
    slot_mask = got_valid[None, None, :]
    scores = jnp.where(slot_mask, scores, -1e30)
    top_score = jnp.max(scores, axis=-1, keepdims=True)
    raised = jnp.where(slot_mask, jnp.exp(scores - top_score), 0.0)
    probabilities = (raised / jnp.sum(raised, axis=-1, keepdims=True)).astype(jnp.bfloat16)
    attended = jnp.einsum(
        "htr,hdr->thd", probabilities, value_heads, preferred_element_type=jnp.float32
    )
    attended = attended.astype(jnp.bfloat16).reshape(targets, head_cols)
    partial = jnp.dot(attended, attn_out, preferred_element_type=jnp.float32).astype(jnp.bfloat16)
    partial = partial.reshape(models, targets // models, width)
    shares_out = lax.all_to_all(partial, MDL, 0, 0, tiled=True)
    return jnp.sum(shares_out.astype(jnp.float32), axis=0).astype(jnp.bfloat16)


def solution(mesh):
    fine = Mesh(mesh.devices.reshape(-1, 2, 4, 8), ("y", "core", "x", "z"))
    in_specs = (
        P(GRP, MDL),
        P(),
        P(GRP, MDL),
        P(MDL, GRP),
        P(),
        P(None, None, MDL),
        P(GRP, MDL),
        P(MDL, None),
        P(),
    )
    out_specs = P(GRP + MDL, None)
    return jax.shard_map(local, mesh=fine, in_specs=in_specs, out_specs=out_specs, check_vma=False)
```

```python
import jax
import jax.numpy as jnp
from jax import lax
from jax.sharding import Mesh, PartitionSpec as P

HEAD_DIM = 128
GRP = ("y", "core")
MDL = ("x", "z")


def swap_cores(value):
    return lax.ppermute(value, "core", [(0, 1), (1, 0)])


def normalize_columns(states, gain):
    wide = states.astype(jnp.float32)
    factor = lax.rsqrt(jnp.mean(wide * wide, axis=0, keepdims=True) + 1e-06)
    return (wide * factor * gain.astype(jnp.float32)[:, None]).astype(jnp.bfloat16)


def spread(value, axes):
    copies = jnp.broadcast_to(value[None], (lax.axis_size(axes),) + value.shape)
    return lax.all_to_all(copies, axes, 0, 0, tiled=True).reshape(-1, value.shape[-1])


def shift(value, step):
    size = lax.axis_size("x")
    return lax.ppermute(value, "x", [(i, (i + step) % size) for i in range(size)])


def slot_plan(row_question, rows_local, groups, my_group):
    capacity = 3 * rows_local // groups
    owners = row_question.reshape(groups, rows_local)
    questions = jnp.arange(groups, dtype=jnp.int32)
    counts = jnp.sum((owners[:, :, None] == questions).astype(jnp.int32), axis=1)
    slots = jnp.arange(capacity, dtype=jnp.int32)
    mine = lax.dynamic_index_in_dim(owners, my_group, 0, keepdims=False)
    sent_counts = lax.dynamic_index_in_dim(counts, my_group, 0, keepdims=False)
    sent_starts = jnp.sum((mine[None, :] < questions[:, None]).astype(jnp.int32), axis=1)
    source = jnp.where(
        slots[None, :] < sent_counts[:, None], sent_starts[:, None] + slots[None, :], -1
    )
    got_counts = lax.dynamic_index_in_dim(counts, my_group, 1, keepdims=False)
    got_valid = (slots[None, :] < got_counts[:, None]).reshape(-1)
    rows = jnp.arange(rows_local, dtype=jnp.int32)
    pick = (rows[:, None] == source.reshape(1, -1)).astype(jnp.bfloat16)
    return capacity, pick, got_valid


def local(
    row_states, ffn_gain, ffn_in, ffn_out, final_gain, kv_weight, queries, attn_out, row_question
):
    groups = lax.axis_size(GRP)
    models = lax.axis_size(MDL)
    my_group = lax.axis_index(GRP)
    my_core = lax.axis_index("core")
    rows_local, feats_local = row_states.shape
    hid_local = ffn_in.shape[1]
    width = feats_local * models

    own_rows = row_states.T
    both = jnp.concatenate([ffn_in, ffn_out.T], axis=1)
    both_half = lax.all_gather(both, "y", axis=0, tiled=True)
    both_other = swap_cores(both_half)
    in_half, out_half = both_half[:, :hid_local], both_half[:, hid_local:]
    in_other, out_other = both_other[:, :hid_local], both_other[:, hid_local:]
    full_rows = spread(own_rows, MDL)
    normed = normalize_columns(full_rows, ffn_gain)
    halves = normed.reshape(-1, 2, ffn_in.shape[0], rows_local)
    mine = lax.dynamic_index_in_dim(halves, my_core, 1, keepdims=False).reshape(-1, rows_local)
    theirs = lax.dynamic_index_in_dim(halves, 1 - my_core, 1, keepdims=False)
    theirs = theirs.reshape(-1, rows_local)

    def contract(weight, columns):
        return lax.dot_general(
            weight, columns, (((0,), (0,)), ((), ())), preferred_element_type=jnp.float32
        )

    pre_active = contract(in_half, mine) + contract(in_other, theirs)
    hidden = jnp.maximum(pre_active, 0.0).astype(jnp.bfloat16)
    share_mine = jnp.dot(out_half, hidden, preferred_element_type=jnp.float32)
    share_other = jnp.dot(out_other, hidden, preferred_element_type=jnp.float32)
    share_mine = share_mine.astype(jnp.bfloat16).reshape(-1, 1, ffn_out.shape[1], rows_local)
    share_other = share_other.astype(jnp.bfloat16).reshape(-1, 1, ffn_out.shape[1], rows_local)
    first = my_core == 0
    shares = jnp.concatenate(
        [
            jnp.where(first, share_mine, share_other),
            jnp.where(first, share_other, share_mine),
        ],
        axis=1,
    ).reshape(models, feats_local, rows_local)
    arrived = lax.all_to_all(shares, MDL, 0, 0, tiled=True)
    ffn_sum = jnp.sum(arrived.astype(jnp.float32), axis=0)
    enc_state = (own_rows.astype(jnp.float32) + ffn_sum).astype(jnp.bfloat16)

    capacity, pick, got_valid = slot_plan(row_question, rows_local, groups, my_group)
    packed = jnp.dot(enc_state, pick, preferred_element_type=jnp.float32).astype(jnp.bfloat16)
    packed = packed.reshape(feats_local, groups, capacity).transpose(1, 0, 2)
    regrouped = lax.all_to_all(packed, GRP, 0, 0, tiled=True)
    slots = regrouped.transpose(1, 0, 2).reshape(feats_local, groups * capacity)
    near = spread(slots, "z")
    behind, ahead = shift(near, 1), shift(near, -1)
    half = near.shape[0] // 2
    far = jnp.concatenate([shift(behind[:half], 1), shift(ahead[half:], -1)], axis=0)
    slot_rows = jnp.concatenate([near, behind, ahead, far], axis=0)
    my_x = lax.axis_index("x")
    ring = [(my_x + step) % lax.axis_size("x") for step in (0, 3, 1, 2)]
    gains = final_gain.reshape(len(ring), -1)
    turned_gain = jnp.concatenate([lax.dynamic_index_in_dim(gains, i, 0, False) for i in ring])
    banks = kv_weight.reshape(2, len(ring), -1, kv_weight.shape[2])
    turned = jnp.concatenate([lax.dynamic_index_in_dim(banks, i, 1, False) for i in ring], axis=1)
    encoded = normalize_columns(slot_rows, turned_gain)

    projected = lax.dot_general(
        turned, encoded, (((1,), (0,)), ((), ())), preferred_element_type=jnp.float32
    ).astype(jnp.bfloat16)
    head_cols = kv_weight.shape[2]
    heads_local = head_cols // HEAD_DIM
    targets = queries.shape[0]
    key_heads = projected[0].reshape(heads_local, HEAD_DIM, -1)
    value_heads = projected[1].reshape(heads_local, HEAD_DIM, -1)
    query_heads = queries.reshape(targets, heads_local, HEAD_DIM)
    scores = jnp.einsum("thd,hdr->htr", query_heads, key_heads, preferred_element_type=jnp.float32)
    slot_mask = got_valid[None, None, :]
    scores = jnp.where(slot_mask, scores, -1e30)
    top_score = jnp.max(scores, axis=-1, keepdims=True)
    raised = jnp.where(slot_mask, jnp.exp(scores - top_score), 0.0)
    probabilities = (raised / jnp.sum(raised, axis=-1, keepdims=True)).astype(jnp.bfloat16)
    attended = jnp.einsum(
        "htr,hdr->thd", probabilities, value_heads, preferred_element_type=jnp.float32
    )
    attended = attended.astype(jnp.bfloat16).reshape(targets, head_cols)
    partial = jnp.dot(attended, attn_out, preferred_element_type=jnp.float32).astype(jnp.bfloat16)
    partial = partial.reshape(models, targets // models, width)
    shares_out = lax.all_to_all(partial, MDL, 0, 0, tiled=True)
    return jnp.sum(shares_out.astype(jnp.float32), axis=0).astype(jnp.bfloat16)


def solution(mesh):
    fine = Mesh(mesh.devices.reshape(-1, 2, 4, 8), ("y", "core", "x", "z"))
    in_specs = (
        P(GRP, MDL),
        P(),
        P(GRP, MDL),
        P(MDL, GRP),
        P(),
        P(None, None, MDL),
        P(GRP, MDL),
        P(MDL, None),
        P(),
    )
    out_specs = P(GRP + MDL, None)
    return jax.shard_map(local, mesh=fine, in_specs=in_specs, out_specs=out_specs, check_vma=False)
```

```python
import jax
import jax.numpy as jnp
from jax import lax
from jax.experimental import pallas as pl
from jax.experimental.pallas import tpu as pltpu
from jax.sharding import Mesh, PartitionSpec as P

HEAD_DIM = 128
GRP = ("y", "core")
MDL = ("x", "z")


def swap_cores(value):
    return lax.ppermute(value, "core", [(0, 1), (1, 0)])


def spread(value, axes):
    copies = jnp.broadcast_to(value[None], (lax.axis_size(axes),) + value.shape)
    return lax.all_to_all(copies, axes, 0, 0, tiled=True).reshape(-1, value.shape[-1])


def shift(value, axis, step):
    size = lax.axis_size(axis)
    return lax.ppermute(value, axis, [(i, (i + step) % size) for i in range(size)])


def ring_gather(value, axis, beside):
    size = lax.axis_size(axis)
    blocks, steps = [value], [0]
    up = down = value
    for step in range(1, size // 2):
        up, down = shift(up, axis, 1), shift(down, axis, -1)
        blocks += [up, down]
        steps += [size - step, step]
    up, beside = lax.optimization_barrier((up, beside))
    blocks.append(shift(up, axis, 1))
    steps.append(size // 2)
    return blocks, steps, beside


def slot_plan(row_question, rows_local, groups, my_group):
    capacity = 3 * rows_local // groups
    owners = row_question.reshape(groups, rows_local)
    questions = jnp.arange(groups, dtype=jnp.int32)
    counts = jnp.sum((owners[:, :, None] == questions).astype(jnp.int32), axis=1)
    slots = jnp.arange(capacity, dtype=jnp.int32)
    mine = lax.dynamic_index_in_dim(owners, my_group, 0, keepdims=False)
    sent_counts = lax.dynamic_index_in_dim(counts, my_group, 0, keepdims=False)
    sent_starts = jnp.sum((mine[None, :] < questions[:, None]).astype(jnp.int32), axis=1)
    source = jnp.where(
        slots[None, :] < sent_counts[:, None], sent_starts[:, None] + slots[None, :], -1
    )
    got_counts = lax.dynamic_index_in_dim(counts, my_group, 1, keepdims=False)
    got_valid = (slots[None, :] < got_counts[:, None]).reshape(-1)
    rows = jnp.arange(rows_local, dtype=jnp.int32)
    pick = (rows[:, None] == source.reshape(1, -1)).astype(jnp.bfloat16)
    return capacity, pick, got_valid


def ffn_kernel(order_ref, core_ref, rows_ref, gain_ref, own_ref, other_ref, out_ref, normed, own_rows, other_rows, hidden):
    width, columns = rows_ref.shape
    piece = own_ref.shape[0] // order_ref.shape[0]
    hid = hidden.shape[1]
    wide = rows_ref[...].astype(jnp.float32)
    factor = lax.rsqrt(jnp.sum(wide * wide, axis=0, keepdims=True) * (1.0 / width) + 1e-06)
    normed[...] = (wide * factor * gain_ref[...]).astype(jnp.bfloat16)
    core = core_ref[0]
    for spot in range(order_ref.shape[0]):
        base = order_ref[spot] * (2 * piece)
        mine = pl.multiple_of(base + core * piece, piece)
        theirs = pl.multiple_of(base + (1 - core) * piece, piece)
        own_rows[spot * piece : (spot + 1) * piece, :] = normed[pl.ds(mine, piece), :]
        other_rows[spot * piece : (spot + 1) * piece, :] = normed[pl.ds(theirs, piece), :]
    over_first = (((0,), (0,)), ((), ()))
    over_last = (((1,), (1,)), ((), ()))
    for start in range(0, hid, 256):
        part = lax.dot_general(
            own_rows[...], own_ref[:, start : start + 256], over_first,
            preferred_element_type=jnp.float32,
        ) + lax.dot_general(
            other_rows[...], other_ref[:, start : start + 256], over_first,
            preferred_element_type=jnp.float32,
        )
        hidden[:, start : start + 256] = jnp.maximum(part, 0.0).astype(jnp.bfloat16)
    for weight_ref, shift_by in ((own_ref, core), (other_ref, 1 - core)):
        share = lax.dot_general(
            weight_ref[:, hid:], hidden[...], over_last, preferred_element_type=jnp.float32
        ).astype(jnp.bfloat16)
        for spot in range(order_ref.shape[0]):
            at = pl.multiple_of(order_ref[spot] * (2 * piece) + shift_by * piece, piece)
            out_ref[pl.ds(at, piece), :] = share[spot * piece : (spot + 1) * piece, :]


def ffn_shares(order, core, rows, gain, own, other):
    width, columns = rows.shape
    hid = own.shape[1] // 2
    smem = pl.BlockSpec(memory_space=pltpu.SMEM)
    vmem = pl.BlockSpec(memory_space=pltpu.VMEM)
    return pl.pallas_call(
        ffn_kernel,
        out_shape=jax.ShapeDtypeStruct((width, columns), jnp.bfloat16),
        in_specs=[smem, smem, vmem, vmem, vmem, vmem],
        out_specs=vmem,
        scratch_shapes=[
            pltpu.VMEM((width, columns), jnp.bfloat16),
            pltpu.VMEM((width // 2, columns), jnp.bfloat16),
            pltpu.VMEM((width // 2, columns), jnp.bfloat16),
            pltpu.VMEM((columns, hid), jnp.bfloat16),
        ],
        cost_estimate=pl.CostEstimate(
            flops=4 * width * hid * columns, transcendentals=columns, bytes_accessed=12 << 20
        ),
        name="ffn_shares",
    )(order, core, rows, gain, own, other)


def attend_kernel(
    order_ref, near_ref, behind_ref, ahead_ref, low_ref, high_ref, kv_ref, q_ref, out_w_ref,
    valid_ref, out_ref, total, factor_ref,
):
    head = pl.program_id(0)
    quarter, slots = near_ref.shape
    half = quarter // 2
    width = 4 * quarter

    @pl.when(head == 0)
    def _():
        squares = jnp.zeros((1, slots), jnp.float32)
        for ref in (near_ref, behind_ref, ahead_ref, low_ref, high_ref):
            wide = ref[...].astype(jnp.float32)
            squares += jnp.sum(wide * wide, axis=0, keepdims=True)
        factor_ref[...] = lax.rsqrt(squares * (1.0 / width) + 1e-06)

    near_at = pl.multiple_of(order_ref[0] * quarter, quarter)
    behind_at = pl.multiple_of(order_ref[1] * quarter, quarter)
    ahead_at = pl.multiple_of(order_ref[2] * quarter, quarter)
    low_at = pl.multiple_of(order_ref[3] * quarter, quarter)
    high_at = pl.multiple_of(order_ref[3] * quarter + half, half)

    def project(kind):
        parts = [
            jnp.dot(kv_ref[kind, :, pl.ds(at, size)], ref[...], preferred_element_type=jnp.float32)
            for ref, at, size in (
                (near_ref, near_at, quarter),
                (behind_ref, behind_at, quarter),
                (ahead_ref, ahead_at, quarter),
                (low_ref, low_at, half),
                (high_ref, high_at, half),
            )
        ]
        whole = parts[0] + parts[1] + parts[2] + parts[3] + parts[4]
        return (whole * factor_ref[...]).astype(jnp.bfloat16)

    scores = jnp.dot(q_ref[...], project(0), preferred_element_type=jnp.float32)
    valid = valid_ref[...] > 0.0
    scores = jnp.where(valid, scores, -1e30)
    top = jnp.max(scores, axis=-1, keepdims=True)
    raised = jnp.where(valid, jnp.exp(scores - top), 0.0)
    weight = 1.0 / jnp.sum(raised, axis=-1, keepdims=True)
    probabilities = (raised * weight).astype(jnp.bfloat16)
    attended = lax.dot_general(
        probabilities, project(1), (((1,), (1,)), ((), ())), preferred_element_type=jnp.float32
    ).astype(jnp.bfloat16)
    share = jnp.dot(attended, out_w_ref[...], preferred_element_type=jnp.float32)

    @pl.when(head == 0)
    def _():
        total[...] = share

    @pl.when(head > 0)
    def _():
        total[...] += share

    @pl.when(head == pl.num_programs(0) - 1)
    def _():
        out_ref[...] = total[...].astype(jnp.bfloat16)


def attend(order, near, behind, ahead, low, high, kv_rows, queries, attn_out, valid):
    targets, head_cols = queries.shape
    heads = head_cols // HEAD_DIM
    quarter, slots = near.shape
    width = attn_out.shape[1]

    def whole(array):
        return pl.BlockSpec(array.shape, lambda h: (0,) * array.ndim, pipeline_mode=pl.Buffered(1))

    return pl.pallas_call(
        attend_kernel,
        grid=(heads,),
        out_shape=jax.ShapeDtypeStruct((targets, width), jnp.bfloat16),
        in_specs=[
            pl.BlockSpec(memory_space=pltpu.SMEM),
            *[whole(array) for array in (near, behind, ahead, low, high)],
            pl.BlockSpec((2, HEAD_DIM, kv_rows.shape[2]), lambda h: (0, h, 0)),
            pl.BlockSpec((targets, HEAD_DIM), lambda h: (0, h)),
            pl.BlockSpec((HEAD_DIM, width), lambda h: (h, 0)),
            whole(valid),
        ],
        out_specs=pl.BlockSpec((targets, width), lambda h: (0, 0)),
        scratch_shapes=[
            pltpu.VMEM((targets, width), jnp.float32),
            pltpu.VMEM((1, slots), jnp.float32),
        ],
        compiler_params=pltpu.CompilerParams(dimension_semantics=("arbitrary",)),
        cost_estimate=pl.CostEstimate(
            flops=4 * slots * width * head_cols + 4 * slots * targets * head_cols,
            transcendentals=targets * slots * heads,
            bytes_accessed=6 << 20,
        ),
        name="attend",
    )(order, near, behind, ahead, low, high, kv_rows, queries, attn_out, valid)


def local(
    row_states, ffn_gain, ffn_in, ffn_out, final_gain, kv_weight, queries, attn_out, row_question
):
    groups = lax.axis_size(GRP)
    models = lax.axis_size(MDL)
    my_group = lax.axis_index(GRP)
    my_core = lax.axis_index("core")
    rows_local, feats_local = row_states.shape
    width = feats_local * models

    own_rows = row_states.T
    both = jnp.concatenate([ffn_in, ffn_out.T], axis=1)
    blocks, steps, full_rows = ring_gather(both, "y", spread(own_rows, MDL))
    both_half = jnp.concatenate(blocks, axis=0)
    both_other = swap_cores(both_half)
    y_size = lax.axis_size("y")
    y_order = (lax.axis_index("y") + jnp.array(steps, jnp.int32)) % y_size
    shares = ffn_shares(
        y_order,
        my_core.reshape(1),
        full_rows,
        ffn_gain.astype(jnp.float32)[:, None],
        both_half,
        both_other,
    ).reshape(models, feats_local, rows_local)
    arrived = lax.all_to_all(shares, MDL, 0, 0, tiled=True)
    ffn_sum = jnp.sum(arrived.astype(jnp.float32), axis=0)
    enc_state = (own_rows.astype(jnp.float32) + ffn_sum).astype(jnp.bfloat16)

    capacity, pick, got_valid = slot_plan(row_question, rows_local, groups, my_group)
    packed = jnp.dot(enc_state, pick, preferred_element_type=jnp.float32).astype(jnp.bfloat16)
    packed = packed.reshape(feats_local, groups, capacity).transpose(1, 0, 2)
    regrouped = lax.all_to_all(packed, GRP, 0, 0, tiled=True)
    slots = regrouped.transpose(1, 0, 2).reshape(feats_local, groups * capacity)
    near = spread(slots, "z")
    behind, ahead = shift(near, "x", 1), shift(near, "x", -1)
    half = near.shape[0] // 2
    far_low, far_high = shift(behind[:half], "x", 1), shift(ahead[half:], "x", -1)
    x_order = (lax.axis_index("x") + jnp.array([0, 3, 1, 2], jnp.int32)) % lax.axis_size("x")
    gained = kv_weight.astype(jnp.float32) * final_gain.astype(jnp.float32)[None, :, None]
    kv_rows = gained.astype(jnp.bfloat16).transpose(0, 2, 1)
    partial = attend(
        x_order,
        near,
        behind,
        ahead,
        far_low,
        far_high,
        kv_rows,
        queries,
        attn_out,
        got_valid.astype(jnp.float32)[None, :],
    )
    partial = partial.reshape(models, queries.shape[0] // models, width)
    shares_out = lax.all_to_all(partial, MDL, 0, 0, tiled=True)
    return jnp.sum(shares_out.astype(jnp.float32), axis=0).astype(jnp.bfloat16)


def solution(mesh):
    fine = Mesh(mesh.devices.reshape(-1, 2, 4, 8), ("y", "core", "x", "z"))
    in_specs = (
        P(GRP, MDL),
        P(),
        P(GRP, MDL),
        P(MDL, GRP),
        P(),
        P(None, None, MDL),
        P(GRP, MDL),
        P(MDL, None),
        P(),
    )
    out_specs = P(GRP + MDL, None)
    return jax.shard_map(local, mesh=fine, in_specs=in_specs, out_specs=out_specs, check_vma=False)
```
